32 devices in a mesh: grp: 4 (over z), mem: 8 (over y, x, core).
Axes of the slice: x: 2, y: 2, z: 4, core: 2. Of those that a mesh axis runs over, the one named last changes fastest.
Arguments:
- basis: float32 [20, 2048, 128], P(None, ('grp', 'mem'))
- precond: bfloat16 [2048, 128, 128], P(('grp', 'mem'))
- leaf_rows: float32 [1024, 128], P(('grp', 'mem')), may hold values from -6 to 6
- leaf_fiber: int32 [1024], P(('grp', 'mem')), may hold values from 0 to 63
- strad_rows: float32 [1024, 128], P(('grp', 'mem')), may hold values from -6 to 6
- strad_fiber: int32 [1024], P(('grp', 'mem')), may hold values from 0 to 63
- strad_count: int32 [32, 4], P(('grp', 'mem')), may hold values from 0 to 8, as said below
Outputs:
- coeffs: float32 [21], replicated
- next_vector: float32 [2048, 128], P(('grp', 'mem'))
The draws below stay inside these ranges and needn't reach their ends.
Inputs may be any that keep to these rules, and one draw needn't show every extreme that they name: `leaf_fiber`: a destination fiber within the destination device. `strad_fiber`: a fiber of the receiving device. The first strad_count slots of a block are live, the rest are not read; some device fills a block.
All inputs are finite; a program needn't handle non-finite values.
Results may differ from the reference program's by a relative error of at most 0.0011.
Values sent between devices are 32-bit elements; how exact they have to be, the bound alone decides.
A program may use at most 64 MiB of HBM per device.

```python
import jax
import jax.numpy as jnp
from jax import lax

NODE_DOF = 128
KRYLOV = 20
FIB_DEV = 64
LEAF_CAP = 4
SCAP = 8
FIBERS = 2048
N_GRP = 4
N_MEM = 8


def draw_basis(key, part):
    noise_key = jax.random.fold_in(key, 21)
    shared_key = jax.random.fold_in(key, 22)
    amp_key = jax.random.fold_in(key, 23)
    sign_key = jax.random.fold_in(key, 24)
    rising = 0.6 + 1.2 * jnp.arange(FIBERS, dtype=jnp.float32) / FIBERS
    values = jax.random.normal(noise_key, (KRYLOV, FIBERS, NODE_DOF), jnp.float32)
    shared = jax.random.normal(shared_key, (FIBERS, NODE_DOF), jnp.float32)
    amps = jax.random.uniform(amp_key, (KRYLOV,), jnp.float32, 0.4, 1.0)
    signs = (2 * jax.random.randint(sign_key, (KRYLOV,), 0, 2) - 1).astype(jnp.float32)
    loads = amps * signs
    mixed = values + loads[:, None, None] * shared[None]
    return mixed * rising[None, :, None]


def draw_precond(key, part):
    first = jax.random.fold_in(key, 11)
    second = jax.random.fold_in(key, 12)
    index = jnp.arange(NODE_DOF)
    identity = (index[:, None] == index[None, :]).astype(jnp.float32)
    diagonal = jax.random.uniform(first, (FIBERS, NODE_DOF, 1), jnp.float32, 0.5, 1.5)
    spread = jax.random.normal(second, (FIBERS, NODE_DOF, NODE_DOF), jnp.float32) * (0.5 / NODE_DOF ** 0.5)
    blocks = identity[None] * diagonal + spread
    return blocks.astype(jnp.bfloat16)


def draw_strad_count(key, part):
    drawn = jax.random.randint(key, (N_GRP * N_MEM, N_GRP), 0, SCAP + 1)
    marker = jnp.arange(N_GRP * N_MEM)[:, None] + jnp.arange(N_GRP)[None, :]
    return jnp.where(marker % 5 == 0, SCAP, drawn).astype(jnp.int32)


def with_ends(result, rng, least, largest):
    longest = result.shape.index(max(result.shape))
    spots = []
    for shift in (0, 1):
        where = [jax.random.randint(jax.random.fold_in(rng, axis), (), 0, length) for axis, length in enumerate(result.shape)]
        where[longest] = (where[longest] + shift) % result.shape[longest]
        spots.append(tuple(where))
    return result.at[spots[0]].set(least).at[spots[1]].set(largest)


def shard_levels(key, dims, cuts, low, top_value):
    def one(position, blocks):
        steps = jax.random.uniform(jax.random.fold_in(jax.random.fold_in(key, 6), position), (blocks,), jnp.float32, low / len(cuts), top_value / len(cuts))
        return jnp.repeat(jnp.exp(steps), dims[position] // blocks).reshape((-1,) + (1,) * (len(dims) - position - 1))

    loudness = one(*cuts[0])
    for cut in cuts[1:]:
        loudness = loudness * one(*cut)
    return loudness


def gaussian(stream_key, dims, width, reach, pieces=(), kind=jnp.bfloat16):
    level = shard_levels(stream_key, dims, pieces, -0.22, 0.18) if pieces else 1.0
    values = jax.random.normal(stream_key, dims, jnp.float32) * width * level
    return jnp.minimum(jnp.maximum(values, -reach), reach).astype(kind)


def setup_inputs(seed: int = 0) -> dict:
    streams_of = jax.random.split(jax.random.key(seed), 8)
    basis = draw_basis(jax.random.fold_in(streams_of[7], 71), 0)
    precond = draw_precond(jax.random.fold_in(streams_of[7], 71), 0)
    leaf_rows = gaussian(streams_of[2], (N_GRP * N_MEM * N_MEM * LEAF_CAP, NODE_DOF), 1.0, 6.0, ((0, 32),), jnp.float32)
    leaf_fiber = with_ends(jax.random.randint(streams_of[3], (N_GRP * N_MEM * N_MEM * LEAF_CAP,), 0, FIB_DEV), jax.random.fold_in(streams_of[3], 1), 0, FIB_DEV - 1).astype(jnp.int32)
    strad_rows = gaussian(streams_of[4], (N_GRP * N_MEM * N_GRP * SCAP, NODE_DOF), 1.0, 6.0, ((0, 32),), jnp.float32)
    strad_fiber = with_ends(jax.random.randint(streams_of[5], (N_GRP * N_MEM * N_GRP * SCAP,), 0, FIB_DEV), jax.random.fold_in(streams_of[5], 1), 0, FIB_DEV - 1).astype(jnp.int32)
    strad_count = draw_strad_count(jax.random.fold_in(streams_of[7], 71), 0)
    return {"basis": basis, "precond": precond, "leaf_rows": leaf_rows, "leaf_fiber": leaf_fiber, "strad_rows": strad_rows, "strad_fiber": strad_fiber, "strad_count": strad_count}


EPS = 1e-06

def reference(basis, precond, leaf_rows, leaf_fiber, strad_rows, strad_fiber, strad_count):
    groups = N_GRP
    members = N_MEM
    slot = jnp.arange(groups * members * members * LEAF_CAP, dtype=jnp.int32)
    group_of = slot // (members * members * LEAF_CAP)
    member_to = slot // LEAF_CAP % members
    target = (group_of * members + member_to) * FIB_DEV + leaf_fiber
    far = jax.ops.segment_sum(leaf_rows, target, num_segments=FIBERS)
    sslot = jnp.arange(groups * members * groups * SCAP, dtype=jnp.int32)
    source_group = sslot // (members * groups * SCAP)
    member = sslot // (groups * SCAP) % members
    dest_group = sslot // SCAP % groups
    within = sslot % SCAP
    arranged = strad_fiber.reshape(groups, members, groups, SCAP).transpose(2, 1, 0, 3).reshape(-1)
    count = strad_count[source_group * members + member, dest_group]
    live = (within < count).astype(jnp.float32)
    near = jax.ops.segment_sum(strad_rows * live[:, None], (dest_group * members + member) * FIB_DEV + arranged, num_segments=FIBERS)
    field = (basis[KRYLOV - 1] + far + near).astype(jnp.bfloat16)

    def apply_block(pair):
        blocks, values = pair
        return jnp.einsum('fij,fj->fi', blocks.astype(jnp.float32), values.astype(jnp.float32), precision=lax.Precision.HIGHEST)
    applied = lax.map(apply_block, (precond.reshape(groups * members, FIB_DEV, NODE_DOF, NODE_DOF), field.reshape(groups * members, FIB_DEV, NODE_DOF)))
    applied = applied.reshape(FIBERS, NODE_DOF)
    total = float(FIBERS * NODE_DOF)
    coef = jnp.einsum('kfi,fi->k', basis, applied, precision=lax.Precision.HIGHEST) / total
    residual = applied - jnp.einsum('k,kfi->fi', coef, basis, precision=lax.Precision.HIGHEST)
    beta = jnp.sqrt(jnp.sum(residual * residual) / total + EPS)
    return (jnp.concatenate([coef, beta[None]]), residual / beta)
```

```python
import functools

import jax
import jax.numpy as jnp
from jax import lax
from jax.experimental import pallas as pl
from jax.experimental.pallas import tpu as pltpu
from jax.sharding import PartitionSpec as P

EPS = 1e-06
MESH = pl.DeviceIdType.MESH
NT = (((1,), (1,)), ((), ()))
TN = (((0,), (0,)), ((), ()))


def iota(shape, axis):
    return lax.broadcasted_iota(jnp.int32, shape, axis)


def row_to_column(row, rows):
    shape = (rows, row.shape[1])
    diagonal = iota(shape, 0) == iota(shape, 1)
    return jnp.sum(jnp.where(diagonal, row, 0.0), axis=1, keepdims=True)


def split3(x):
    high = x.astype(jnp.bfloat16)
    rest = x - high.astype(jnp.float32)
    mid = rest.astype(jnp.bfloat16)
    low = (rest - mid.astype(jnp.float32)).astype(jnp.bfloat16)
    return high, mid, low


def kernel(
    groups, members, krylov, fibers, total,
    basis_h, precond_h, leaf_h, leaf_id_h, strad_h, strad_id_h, count_h,
    coef_ref, next_ref,
    basis, precond, leaf, leaf_id, strad, strad_id, count,
    leaf_out, leaf_in, strad_out, strad_in,
    gram_out, gram_in, gram2_out, gram2_in, dots_out, dots_in,
    field_ref, local_sem, sem,
):
    g, m = lax.axis_index("grp"), lax.axis_index("mem")
    devices = groups * members
    me = g * members + m
    width = basis.shape[1]
    cap = leaf.shape[0] // members
    slots = strad.shape[0] // groups

    barrier = pltpu.get_barrier_semaphore()
    mates = [lax.rem(m + o, members) for o in range(1, members)]
    peers = [lax.rem(g + o, groups) for o in range(1, groups)]
    for mate in mates:
        pl.semaphore_signal(barrier, inc=1, device_id=(g, mate), device_id_type=MESH)
    for peer in peers:
        pl.semaphore_signal(barrier, inc=1, device_id=(peer, m), device_id_type=MESH)

    loads = [
        pltpu.make_async_copy(src, dst, local_sem.at[i])
        for i, (src, dst) in enumerate(
            [
                (leaf_h, leaf), (leaf_id_h, leaf_id), (strad_h, strad),
                (count_h, count), (strad_id_h, strad_id),
                (basis_h, basis), (precond_h, precond),
            ]
        )
    ]
    for load in loads:
        load.start()
    for load in loads[:5]:
        load.wait()

    leaf_rows = leaf.shape[0]
    ids = jnp.broadcast_to(
        row_to_column(leaf_id[...].astype(jnp.float32), leaf_rows), (leaf_rows, width)
    )
    rows = leaf[...]
    for d in range(members):
        leaf_out[d, :cap, :] = rows[d * cap:(d + 1) * cap]
        leaf_out[d, cap:, :] = ids[d * cap:(d + 1) * cap]
    strad_rows = strad.shape[0]
    shape = (strad_rows, groups)
    of_group = iota(shape, 0) // slots == iota(shape, 1)
    live = jnp.sum(
        jnp.where(of_group, count[...].astype(jnp.float32), 0.0), axis=1, keepdims=True
    )
    within = (iota((strad_rows, 1), 0) % slots).astype(jnp.float32)
    kept = jnp.where(within < live, strad[...], 0.0)
    strad_out[...] = kept.reshape(groups, slots, width)
    leaf_in[m] = leaf_out[m]
    strad_in[g] = strad_out[g]
    strad_column = row_to_column(strad_id[...].astype(jnp.float32), strad_rows)
    fiber = iota((1, fibers), 1).astype(jnp.float32)
    strad_sel = (strad_column == fiber).astype(jnp.bfloat16)

    pl.semaphore_wait(barrier, members - 1 + groups - 1)

    def send(src, dst, pair, device):
        pltpu.make_async_remote_copy(
            src_ref=src, dst_ref=dst, send_sem=sem.at[pair], recv_sem=sem.at[pair + 1],
            device_id=device, device_id_type=MESH,
        ).start()

    def wait_bytes(ref, i):
        pltpu.make_async_copy(ref, ref, sem.at[i]).wait()

    for peer in peers[::-1]:
        send(strad_out.at[peer], strad_in.at[g], 2, (peer, m))
    for mate in mates[::-1]:
        send(leaf_out.at[mate], leaf_in.at[m], 0, (g, mate))

    loads[5].wait()
    step = 8
    tiles = pl.cdiv(krylov, 8)
    padded = tiles * 8
    lanes = 1 << (padded - 1).bit_length()

    def gram_step(c, acc):
        parts = []
        for j in range(step):
            x = basis[pl.ds(c * step + j, krylov, stride=fibers), :]
            x = jnp.concatenate(
                [x, jnp.zeros((padded - krylov, width), jnp.float32)], axis=0
            )
            parts.append(x)
        x = jnp.concatenate(parts, axis=1)
        high, mid, low = split3(x)
        stack = jnp.concatenate(
            [high.astype(jnp.float32), mid.astype(jnp.float32), low.astype(jnp.float32)], axis=0
        ).astype(jnp.bfloat16)
        return acc + lax.dot_general(stack, stack, NT, preferred_element_type=jnp.float32)

    nine = lax.fori_loop(
        0, fibers // step, gram_step, jnp.zeros((3 * padded, 3 * padded), jnp.float32)
    )
    tall = nine[:padded] + nine[padded:2 * padded] + nine[2 * padded:]
    gram = tall[:, :padded] + tall[:, padded:2 * padded] + tall[:, 2 * padded:]
    gram = jnp.concatenate(
        [gram, jnp.zeros((padded, lanes - padded), jnp.float32)], axis=1
    )
    gram_tile = jnp.concatenate(
        [gram[8 * t:8 * t + 8] for t in range(tiles)], axis=1
    )
    gram_lanes = gram_out.shape[1]
    if gram_lanes > tiles * lanes:
        gram_tile = jnp.concatenate(
            [gram_tile, jnp.zeros((8, gram_lanes - tiles * lanes), jnp.float32)], axis=1
        )
    gram_out[...] = gram_tile
    gram_in[m] = gram_tile
    loads[6].wait()
    for mate in mates[::-1]:
        send(gram_out, gram_in.at[m], 4, (g, mate))

    wait_bytes(leaf_in.at[pl.ds(0, members - 1)], 1)
    wait_bytes(strad_in.at[pl.ds(0, groups - 1)], 3)
    leaf_got = leaf_in[...]
    named = pltpu.roll(leaf_got, cap, 1).reshape(members * 2 * cap, width)[:, :fibers]
    is_row = iota((members * 2 * cap, 1), 0) % (2 * cap) < cap
    leaf_sel = ((named == fiber) & is_row).astype(jnp.float32)
    sel = jnp.concatenate([leaf_sel, strad_sel.astype(jnp.float32)], axis=0)
    got = jnp.concatenate(
        [
            leaf_got.reshape(members * 2 * cap, width),
            strad_in[...].reshape(strad_rows, width),
        ],
        axis=0,
    )
    sel = sel.astype(jnp.bfloat16)
    high, mid, low = split3(got)
    moved = (
        lax.dot_general(sel, high, TN, preferred_element_type=jnp.float32)
        + lax.dot_general(sel, mid, TN, preferred_element_type=jnp.float32)
        + lax.dot_general(sel, low, TN, preferred_element_type=jnp.float32)
    )
    field = basis[(krylov - 1) * fibers:, :] + moved
    field_ref[...] = field.astype(jnp.bfloat16).astype(jnp.float32)

    wait_bytes(gram_in.at[pl.ds(0, members - 1)], 5)
    gram_sum = jnp.sum(gram_in[...], axis=0)
    gram2_out[...] = gram_sum
    gram2_in[g] = gram_sum

    block = 16
    pieces = []
    for t in range(fibers // block):
        tile = field_ref[t * block:(t + 1) * block, :]
        lhs = jnp.concatenate(
            [
                jnp.where(iota((block, width), 0) == j, tile, 0.0).astype(jnp.bfloat16)
                for j in range(block)
            ],
            axis=1,
        )
        rhs = jnp.concatenate([precond[t * block + j] for j in range(block)], axis=1)
        pieces.append(lax.dot_general(lhs, rhs, NT, preferred_element_type=jnp.float32))
    applied = jnp.concatenate(pieces, axis=0)

    sums = []
    for k in range(krylov + 1):
        other = applied if k == krylov else basis[k * fibers:(k + 1) * fibers, :]
        product = jnp.sum((other * applied).reshape(fibers // 8, 8, width), axis=0)
        sums.append(jnp.sum(product, axis=0, keepdims=True))
    rows_of = pl.cdiv(krylov + 1, 8) * 8
    sums.append(jnp.zeros((rows_of - krylov - 1, width), jnp.float32))
    column = jnp.sum(jnp.concatenate(sums, axis=0), axis=1, keepdims=True)
    shape = (rows_of, width)
    dots = jnp.sum(
        jnp.where(iota(shape, 0) == iota(shape, 1), column, 0.0), axis=0, keepdims=True
    )
    dots_out[...] = dots
    dots_in[me] = dots
    for peer in peers[::-1]:
        send(gram2_out, gram2_in.at[g], 6, (peer, m))

    def send_dots(o, carry):
        to = lax.rem(me + devices - o, devices)
        send(dots_out, dots_in.at[me], 8, (to // members, lax.rem(to, members)))
        return carry

    lax.fori_loop(1, devices, send_dots, 0)

    wait_bytes(gram2_in.at[pl.ds(0, groups - 1)], 7)
    gram_all = jnp.sum(gram2_in[...], axis=0) / total
    wait_bytes(dots_in.at[pl.ds(0, devices - 1)], 9)
    dots = jnp.sum(dots_in[...], axis=0) / total

    lane = iota((1, width), 1)
    coef = jnp.where(lane < krylov, dots, 0.0)
    residual = applied
    for k in range(krylov):
        residual = residual - coef[:, k:k + 1] * basis[k * fibers:(k + 1) * fibers, :]
    square = jnp.sum(
        jnp.where(lane == krylov, dots, 0.0) - 2.0 * coef * coef, axis=1, keepdims=True
    )
    short = coef[:, :lanes]
    wide = jnp.concatenate([short] * (gram_lanes // lanes), axis=1)
    at = iota((8, gram_lanes), 1) // lanes
    down = jnp.zeros((8, gram_lanes), jnp.float32)
    for t in range(tiles):
        shape = (8, width)
        picked = jnp.where(iota(shape, 0) + 8 * t == iota(shape, 1), coef, 0.0)
        down = jnp.where(at == t, jnp.sum(picked, axis=1, keepdims=True), down)
    quad = jnp.sum(gram_all * down * wide, axis=0, keepdims=True)
    square = square + jnp.sum(quad, axis=1, keepdims=True)
    beta = jnp.sqrt(square + EPS)
    coef_ref[...] = jnp.where(lane == krylov, beta, coef)[:, :krylov + 1]
    next_ref[...] = residual / beta

    wait_bytes(leaf_out.at[pl.ds(0, members - 1)], 0)
    wait_bytes(strad_out.at[pl.ds(0, groups - 1)], 2)
    wait_bytes(gram_in.at[pl.ds(0, members - 1)], 4)
    wait_bytes(gram2_in.at[pl.ds(0, groups - 1)], 6)
    wait_bytes(dots_in.at[pl.ds(0, devices - 1)], 8)


def local(basis, precond, leaf_rows, leaf_fiber, strad_rows, strad_fiber, strad_count):
    groups = lax.axis_size("grp")
    members = lax.axis_size("mem")
    devices = groups * members
    krylov, fibers, width = basis.shape
    cap = leaf_rows.shape[0] // members
    slots = strad_rows.shape[0] // groups
    tiles = pl.cdiv(krylov, 8)
    lanes = 1 << (tiles * 8 - 1).bit_length()
    gram_lanes = pl.cdiv(tiles * lanes, 128) * 128
    f32, i32 = jnp.float32, jnp.int32
    any_space = pl.BlockSpec(memory_space=pl.ANY)
    vmem = pl.BlockSpec(memory_space=pltpu.VMEM)
    coeffs, vector = pl.pallas_call(
        functools.partial(
            kernel, groups, members, krylov, fibers, float(fibers * width * devices)
        ),
        out_shape=(
            jax.ShapeDtypeStruct((1, krylov + 1), f32),
            jax.ShapeDtypeStruct((fibers, width), f32),
        ),
        in_specs=[any_space] * 7,
        out_specs=(vmem, vmem),
        scratch_shapes=[
            pltpu.VMEM((krylov * fibers, width), f32),
            pltpu.VMEM(precond.shape, precond.dtype),
            pltpu.VMEM(leaf_rows.shape, f32),
            pltpu.VMEM((1, leaf_fiber.shape[0]), i32),
            pltpu.VMEM(strad_rows.shape, f32),
            pltpu.VMEM((1, strad_fiber.shape[0]), i32),
            pltpu.VMEM(strad_count.shape, i32),
            pltpu.VMEM((members, 2 * cap, width), f32),
            pltpu.VMEM((members, 2 * cap, width), f32),
            pltpu.VMEM((groups, slots, width), f32),
            pltpu.VMEM((groups, slots, width), f32),
            pltpu.VMEM((8, gram_lanes), f32),
            pltpu.VMEM((members, 8, gram_lanes), f32),
            pltpu.VMEM((8, gram_lanes), f32),
            pltpu.VMEM((groups, 8, gram_lanes), f32),
            pltpu.VMEM((1, width), f32),
            pltpu.VMEM((devices, 1, width), f32),
            pltpu.VMEM((fibers, width), f32),
            pltpu.SemaphoreType.DMA((7,)),
            pltpu.SemaphoreType.DMA((10,)),
        ],
        compiler_params=pltpu.CompilerParams(collective_id=0, has_side_effects=True),
        name="gmres_step",
    )(
        basis.reshape(krylov * fibers, width), precond, leaf_rows,
        leaf_fiber.reshape(1, -1), strad_rows, strad_fiber.reshape(1, -1), strad_count,
    )
    return coeffs.reshape(krylov + 1), vector


def solution(mesh):
    return jax.shard_map(
        local,
        mesh=mesh,
        in_specs=(
            P(None, ("grp", "mem"), None),
            P(("grp", "mem"), None, None),
            P(("grp", "mem"), None),
            P(("grp", "mem")),
            P(("grp", "mem"), None),
            P(("grp", "mem")),
            P(("grp", "mem"), None),
        ),
        out_specs=(P(), P(("grp", "mem"), None)),
        check_vma=False,
    )
```

```python
import functools

import jax
import jax.numpy as jnp
from jax import lax
from jax.experimental import pallas as pl
from jax.experimental.pallas import tpu as pltpu
from jax.sharding import PartitionSpec as P

EPS = 1e-06
MESH = pl.DeviceIdType.MESH
NT = (((1,), (1,)), ((), ()))
TN = (((0,), (0,)), ((), ()))


def iota(shape, axis):
    return lax.broadcasted_iota(jnp.int32, shape, axis)


def row_to_column(row, rows):
    shape = (rows, row.shape[1])
    diagonal = iota(shape, 0) == iota(shape, 1)
    return jnp.sum(jnp.where(diagonal, row, 0.0), axis=1, keepdims=True)


def split3(x):
    high = x.astype(jnp.bfloat16)
    rest = x - high.astype(jnp.float32)
    mid = rest.astype(jnp.bfloat16)
    low = (rest - mid.astype(jnp.float32)).astype(jnp.bfloat16)
    return high, mid, low


def kernel(
    groups, members, krylov, fibers, total,
    basis_h, precond_h, leaf_h, leaf_id_h, strad_h, strad_id_h, count_h,
    coef_ref, next_ref,
    basis, precond, leaf, leaf_id, strad, strad_id, count,
    leaf_out, leaf_in, strad_out, strad_in,
    gram_out, gram_in, gram2_out, gram2_in, dots_out, dots_in,
    field_ref, local_sem, sem,
):
    g, m = lax.axis_index("grp"), lax.axis_index("mem")
    devices = groups * members
    me = g * members + m
    width = basis.shape[1]
    cap = leaf.shape[0] // members
    slots = strad.shape[0] // groups

    barrier = pltpu.get_barrier_semaphore()
    mates = [lax.rem(m + o, members) for o in range(1, members)]
    peers = [lax.rem(g + o, groups) for o in range(1, groups)]
    for mate in mates:
        pl.semaphore_signal(barrier, inc=1, device_id=(g, mate), device_id_type=MESH)
    for peer in peers:
        pl.semaphore_signal(barrier, inc=1, device_id=(peer, m), device_id_type=MESH)

    loads = [
        pltpu.make_async_copy(src, dst, local_sem.at[i])
        for i, (src, dst) in enumerate(
            [
                (leaf_h, leaf), (leaf_id_h, leaf_id), (strad_h, strad),
                (count_h, count), (strad_id_h, strad_id),
                (basis_h, basis), (precond_h, precond),
            ]
        )
    ]
    for load in loads:
        load.start()
    for load in loads[:5]:
        load.wait()

    leaf_rows = leaf.shape[0]
    ids = jnp.broadcast_to(
        row_to_column(leaf_id[...].astype(jnp.float32), leaf_rows), (leaf_rows, width)
    )
    rows = leaf[...]
    for d in range(members):
        leaf_out[d, :cap, :] = rows[d * cap:(d + 1) * cap]
        leaf_out[d, cap:, :] = ids[d * cap:(d + 1) * cap]
    strad_rows = strad.shape[0]
    shape = (strad_rows, groups)
    of_group = iota(shape, 0) // slots == iota(shape, 1)
    live = jnp.sum(
        jnp.where(of_group, count[...].astype(jnp.float32), 0.0), axis=1, keepdims=True
    )
    within = (iota((strad_rows, 1), 0) % slots).astype(jnp.float32)
    kept = jnp.where(within < live, strad[...], 0.0)
    strad_out[...] = kept.reshape(groups, slots, width)
    leaf_in[m] = leaf_out[m]
    strad_in[g] = strad_out[g]
    strad_column = row_to_column(strad_id[...].astype(jnp.float32), strad_rows)
    fiber = iota((1, fibers), 1).astype(jnp.float32)
    strad_sel = (strad_column == fiber).astype(jnp.bfloat16)

    pl.semaphore_wait(barrier, members - 1 + groups - 1)

    def send(src, dst, pair, device):
        pltpu.make_async_remote_copy(
            src_ref=src, dst_ref=dst, send_sem=sem.at[pair], recv_sem=sem.at[pair + 1],
            device_id=device, device_id_type=MESH,
        ).start()

    def wait_bytes(ref, i):
        pltpu.make_async_copy(ref, ref, sem.at[i]).wait()

    for peer in peers[::-1]:
        send(strad_out.at[peer], strad_in.at[g], 2, (peer, m))
    for mate in mates[::-1]:
        send(leaf_out.at[mate], leaf_in.at[m], 0, (g, mate))

    loads[5].wait()
    step = 8
    tiles = pl.cdiv(krylov, 8)
    padded = tiles * 8
    lanes = 1 << (padded - 1).bit_length()

    def gram_step(c, acc):
        parts = []
        for j in range(step):
            x = basis[pl.ds(c * step + j, krylov, stride=fibers), :]
            x = jnp.concatenate(
                [x, jnp.zeros((padded - krylov, width), jnp.float32)], axis=0
            )
            parts.append(x)
        x = jnp.concatenate(parts, axis=1)
        high, mid, low = split3(x)
        stack = jnp.concatenate(
            [high.astype(jnp.float32), mid.astype(jnp.float32), low.astype(jnp.float32)], axis=0
        ).astype(jnp.bfloat16)
        return acc + lax.dot_general(stack, stack, NT, preferred_element_type=jnp.float32)

    nine = lax.fori_loop(
        0, fibers // step, gram_step, jnp.zeros((3 * padded, 3 * padded), jnp.float32)
    )
    tall = nine[:padded] + nine[padded:2 * padded] + nine[2 * padded:]
    gram = tall[:, :padded] + tall[:, padded:2 * padded] + tall[:, 2 * padded:]
    gram = jnp.concatenate(
        [gram, jnp.zeros((padded, lanes - padded), jnp.float32)], axis=1
    )
    gram_tile = jnp.concatenate(
        [gram[8 * t:8 * t + 8] for t in range(tiles)], axis=1
    )
    gram_lanes = gram_out.shape[1]
    if gram_lanes > tiles * lanes:
        gram_tile = jnp.concatenate(
            [gram_tile, jnp.zeros((8, gram_lanes - tiles * lanes), jnp.float32)], axis=1
        )
    gram_out[...] = gram_tile
    gram_in[m] = gram_tile
    loads[6].wait()
    for mate in mates[::-1]:
        send(gram_out, gram_in.at[m], 4, (g, mate))

    wait_bytes(leaf_in.at[pl.ds(0, members - 1)], 1)
    wait_bytes(strad_in.at[pl.ds(0, groups - 1)], 3)
    leaf_got = leaf_in[...]
    named = pltpu.roll(leaf_got, cap, 1).reshape(members * 2 * cap, width)[:, :fibers]
    is_row = iota((members * 2 * cap, 1), 0) % (2 * cap) < cap
    leaf_sel = ((named == fiber) & is_row).astype(jnp.float32)
    sel = jnp.concatenate([leaf_sel, strad_sel.astype(jnp.float32)], axis=0)
    got = jnp.concatenate(
        [
            leaf_got.reshape(members * 2 * cap, width),
            strad_in[...].reshape(strad_rows, width),
        ],
        axis=0,
    )
    sel = sel.astype(jnp.bfloat16)
    high, mid, low = split3(got)
    moved = (
        lax.dot_general(sel, high, TN, preferred_element_type=jnp.float32)
        + lax.dot_general(sel, mid, TN, preferred_element_type=jnp.float32)
        + lax.dot_general(sel, low, TN, preferred_element_type=jnp.float32)
    )
    field = basis[(krylov - 1) * fibers:, :] + moved
    field_ref[...] = field.astype(jnp.bfloat16).astype(jnp.float32)

    block = 16
    pieces = []
    for t in range(fibers // block):
        tile = field_ref[t * block:(t + 1) * block, :]
        lhs = jnp.concatenate(
            [
                jnp.where(iota((block, width), 0) == j, tile, 0.0).astype(jnp.bfloat16)
                for j in range(block)
            ],
            axis=1,
        )
        rhs = jnp.concatenate([precond[t * block + j] for j in range(block)], axis=1)
        pieces.append(lax.dot_general(lhs, rhs, NT, preferred_element_type=jnp.float32))
    applied = jnp.concatenate(pieces, axis=0)

    sums = []
    for k in range(krylov + 1):
        other = applied if k == krylov else basis[k * fibers:(k + 1) * fibers, :]
        product = jnp.sum((other * applied).reshape(fibers // 8, 8, width), axis=0)
        sums.append(jnp.sum(product, axis=0, keepdims=True))
    rows_of = pl.cdiv(krylov + 1, 8) * 8
    sums.append(jnp.zeros((rows_of - krylov - 1, width), jnp.float32))
    column = jnp.sum(jnp.concatenate(sums, axis=0), axis=1, keepdims=True)
    shape = (rows_of, width)
    dots = jnp.sum(
        jnp.where(iota(shape, 0) == iota(shape, 1), column, 0.0), axis=0, keepdims=True
    )
    dots_out[...] = dots
    dots_in[me] = dots
    if devices <= 64:
        for i in range(groups * members - 1, 0, -1):
            to = (([g] + peers)[i // members], ([m] + mates)[i % members])
            send(dots_out, dots_in.at[me], 8, to)
    else:

        def send_dots(o, carry):
            to = lax.rem(me + devices - o, devices)
            send(dots_out, dots_in.at[me], 8, (to // members, lax.rem(to, members)))
            return carry

        lax.fori_loop(1, devices, send_dots, 0)

    wait_bytes(gram_in.at[pl.ds(0, members - 1)], 5)
    gram_sum = jnp.sum(gram_in[...], axis=0)
    gram2_out[...] = gram_sum
    gram2_in[g] = gram_sum
    for peer in peers[::-1]:
        send(gram2_out, gram2_in.at[g], 6, (peer, m))

    wait_bytes(gram2_in.at[pl.ds(0, groups - 1)], 7)
    gram_all = jnp.sum(gram2_in[...], axis=0) / total
    wait_bytes(dots_in.at[pl.ds(0, devices - 1)], 9)
    dots = jnp.sum(dots_in[...], axis=0) / total

    lane = iota((1, width), 1)
    coef = jnp.where(lane < krylov, dots, 0.0)
    residual = applied
    for k in range(krylov):
        residual = residual - coef[:, k:k + 1] * basis[k * fibers:(k + 1) * fibers, :]
    square = jnp.sum(
        jnp.where(lane == krylov, dots, 0.0) - 2.0 * coef * coef, axis=1, keepdims=True
    )
    short = coef[:, :lanes]
    wide = jnp.concatenate([short] * (gram_lanes // lanes), axis=1)
    at = iota((8, gram_lanes), 1) // lanes
    down = jnp.zeros((8, gram_lanes), jnp.float32)
    for t in range(tiles):
        shape = (8, width)
        picked = jnp.where(iota(shape, 0) + 8 * t == iota(shape, 1), coef, 0.0)
        down = jnp.where(at == t, jnp.sum(picked, axis=1, keepdims=True), down)
    quad = jnp.sum(gram_all * down * wide, axis=0, keepdims=True)
    square = square + jnp.sum(quad, axis=1, keepdims=True)
    beta = jnp.sqrt(square + EPS)
    coef_ref[...] = jnp.where(lane == krylov, beta, coef)[:, :krylov + 1]
    next_ref[...] = residual / beta

    wait_bytes(leaf_out.at[pl.ds(0, members - 1)], 0)
    wait_bytes(strad_out.at[pl.ds(0, groups - 1)], 2)
    wait_bytes(gram_in.at[pl.ds(0, members - 1)], 4)
    wait_bytes(gram2_in.at[pl.ds(0, groups - 1)], 6)
    wait_bytes(dots_in.at[pl.ds(0, devices - 1)], 8)


def put_out(coef_ref, next_ref, coef_h, next_h, sem):
    second = pltpu.make_async_copy(next_ref, next_h, sem.at[1])
    first = pltpu.make_async_copy(coef_ref, coef_h, sem.at[0])
    second.start()
    first.start()
    first.wait()
    second.wait()


def local(basis, precond, leaf_rows, leaf_fiber, strad_rows, strad_fiber, strad_count):
    groups = lax.axis_size("grp")
    members = lax.axis_size("mem")
    devices = groups * members
    krylov, fibers, width = basis.shape
    cap = leaf_rows.shape[0] // members
    slots = strad_rows.shape[0] // groups
    tiles = pl.cdiv(krylov, 8)
    lanes = 1 << (tiles * 8 - 1).bit_length()
    gram_lanes = pl.cdiv(tiles * lanes, 128) * 128
    f32, i32 = jnp.float32, jnp.int32
    any_space = pl.BlockSpec(memory_space=pl.ANY)
    vmem = pl.BlockSpec(memory_space=pltpu.VMEM)
    coeffs, vector = pl.pallas_call(
        functools.partial(
            kernel, groups, members, krylov, fibers, float(fibers * width * devices)
        ),
        out_shape=(
            pltpu.VMEM((1, krylov + 1), f32),
            pltpu.VMEM((fibers, width), f32),
        ),
        in_specs=[any_space] * 7,
        out_specs=(vmem, vmem),
        scratch_shapes=[
            pltpu.VMEM((krylov * fibers, width), f32),
            pltpu.VMEM(precond.shape, precond.dtype),
            pltpu.VMEM(leaf_rows.shape, f32),
            pltpu.VMEM((1, leaf_fiber.shape[0]), i32),
            pltpu.VMEM(strad_rows.shape, f32),
            pltpu.VMEM((1, strad_fiber.shape[0]), i32),
            pltpu.VMEM(strad_count.shape, i32),
            pltpu.VMEM((members, 2 * cap, width), f32),
            pltpu.VMEM((members, 2 * cap, width), f32),
            pltpu.VMEM((groups, slots, width), f32),
            pltpu.VMEM((groups, slots, width), f32),
            pltpu.VMEM((8, gram_lanes), f32),
            pltpu.VMEM((members, 8, gram_lanes), f32),
            pltpu.VMEM((8, gram_lanes), f32),
            pltpu.VMEM((groups, 8, gram_lanes), f32),
            pltpu.VMEM((1, width), f32),
            pltpu.VMEM((devices, 1, width), f32),
            pltpu.VMEM((fibers, width), f32),
            pltpu.SemaphoreType.DMA((7,)),
            pltpu.SemaphoreType.DMA((10,)),
        ],
        compiler_params=pltpu.CompilerParams(collective_id=0, has_side_effects=True),
        name="gmres_step",
    )(
        basis.reshape(krylov * fibers, width), precond, leaf_rows,
        leaf_fiber.reshape(1, -1), strad_rows, strad_fiber.reshape(1, -1), strad_count,
    )
    coeffs, vector = pl.pallas_call(
        put_out,
        out_shape=(
            jax.ShapeDtypeStruct((1, krylov + 1), f32),
            jax.ShapeDtypeStruct((fibers, width), f32),
        ),
        in_specs=[vmem, vmem],
        out_specs=(any_space, any_space),
        scratch_shapes=[pltpu.SemaphoreType.DMA((2,))],
        compiler_params=pltpu.CompilerParams(vmem_limit_bytes=1 << 20),
        name="put_out",
    )(coeffs, vector)
    return coeffs.reshape(krylov + 1), vector


def solution(mesh):
    return jax.shard_map(
        local,
        mesh=mesh,
        in_specs=(
            P(None, ("grp", "mem"), None),
            P(("grp", "mem"), None, None),
            P(("grp", "mem"), None),
            P(("grp", "mem")),
            P(("grp", "mem"), None),
            P(("grp", "mem")),
            P(("grp", "mem"), None),
        ),
        out_specs=(P(), P(("grp", "mem"), None)),
        check_vma=False,
    )
```

```python
import functools

import jax
import jax.numpy as jnp
from jax import lax
from jax.experimental import pallas as pl
from jax.experimental.pallas import tpu as pltpu
from jax.sharding import PartitionSpec as P

EPS = 1e-06
MESH = pl.DeviceIdType.MESH
NT = (((1,), (1,)), ((), ()))
TN = (((0,), (0,)), ((), ()))


def iota(shape, axis):
    return lax.broadcasted_iota(jnp.int32, shape, axis)


def row_to_column(row, rows):
    shape = (rows, row.shape[1])
    diagonal = iota(shape, 0) == iota(shape, 1)
    return jnp.sum(jnp.where(diagonal, row, 0.0), axis=1, keepdims=True)


def split3(x):
    high = x.astype(jnp.bfloat16)
    rest = x - high.astype(jnp.float32)
    mid = rest.astype(jnp.bfloat16)
    low = (rest - mid.astype(jnp.float32)).astype(jnp.bfloat16)
    return high, mid, low


def kernel(
    groups, members, krylov, fibers, total,
    basis_h, precond_h, leaf_h, leaf_id_h, strad_h, strad_id_h, count_h,
    coef_ref, next_ref,
    basis, precond, leaf, leaf_id, strad, strad_id, count,
    leaf_out, leaf_in, strad_out, strad_in,
    gram_out, gram_in, gram2_out, gram2_in, dots_out, dots_in,
    field_ref, turned, local_sem, sem,
):
    g, m = lax.axis_index("grp"), lax.axis_index("mem")
    devices = groups * members
    me = g * members + m
    width = basis.shape[1]
    cap = leaf.shape[0] // members
    slots = strad.shape[0] // groups

    barrier = pltpu.get_barrier_semaphore()
    mates = [lax.rem(m + o, members) for o in range(1, members)]
    peers = [lax.rem(g + o, groups) for o in range(1, groups)]
    for peer in peers:
        pl.semaphore_signal(barrier, inc=1, device_id=(peer, m), device_id_type=MESH)
    for mate in mates:
        pl.semaphore_signal(barrier, inc=1, device_id=(g, mate), device_id_type=MESH)

    loads = [
        pltpu.make_async_copy(src, dst, local_sem.at[i])
        for i, (src, dst) in enumerate(
            [
                (leaf_h, leaf), (leaf_id_h, leaf_id), (strad_h, strad),
                (count_h, count), (strad_id_h, strad_id),
                (basis_h, basis), (precond_h, precond),
            ]
        )
    ]
    for load in loads:
        load.start()
    for load in loads[:5]:
        load.wait()

    leaf_rows = leaf.shape[0]
    ids = jnp.broadcast_to(
        row_to_column(leaf_id[...].astype(jnp.float32), leaf_rows), (leaf_rows, width)
    )
    rows = leaf[...]
    for d in range(members):
        leaf_out[d, :cap, :] = rows[d * cap:(d + 1) * cap]
        leaf_out[d, cap:, :] = ids[d * cap:(d + 1) * cap]
    strad_rows = strad.shape[0]
    shape = (strad_rows, groups)
    of_group = iota(shape, 0) // slots == iota(shape, 1)
    live = jnp.sum(
        jnp.where(of_group, count[...].astype(jnp.float32), 0.0), axis=1, keepdims=True
    )
    within = (iota((strad_rows, 1), 0) % slots).astype(jnp.float32)
    kept = jnp.where(within < live, strad[...], 0.0)
    strad_out[...] = kept.reshape(groups, slots, width)
    leaf_in[m] = leaf_out[m]
    strad_in[g] = strad_out[g]
    strad_column = row_to_column(strad_id[...].astype(jnp.float32), strad_rows)
    fiber = iota((1, fibers), 1).astype(jnp.float32)
    strad_sel = (strad_column == fiber).astype(jnp.bfloat16)

    pl.semaphore_wait(barrier, members - 1 + groups - 1)

    def send(src, dst, pair, device):
        pltpu.make_async_remote_copy(
            src_ref=src, dst_ref=dst, send_sem=sem.at[pair], recv_sem=sem.at[pair + 1],
            device_id=device, device_id_type=MESH,
        ).start()

    def wait_bytes(ref, i):
        pltpu.make_async_copy(ref, ref, sem.at[i]).wait()

    for peer in peers[::-1]:
        send(strad_out.at[peer], strad_in.at[g], 2, (peer, m))
    for mate in mates[::-1]:
        send(leaf_out.at[mate], leaf_in.at[m], 0, (g, mate))

    loads[5].wait()
    step = 8
    tiles = pl.cdiv(krylov, 8)
    padded = tiles * 8
    lanes = 1 << (padded - 1).bit_length()

    def gram_step(c, acc):
        parts = []
        for j in range(step):
            x = basis[pl.ds(c * step + j, krylov, stride=fibers), :]
            x = jnp.concatenate(
                [x, jnp.zeros((padded - krylov, width), jnp.float32)], axis=0
            )
            parts.append(x)
        x = jnp.concatenate(parts, axis=1)
        high, mid, low = split3(x)
        stack = jnp.concatenate(
            [high.astype(jnp.float32), mid.astype(jnp.float32), low.astype(jnp.float32)], axis=0
        ).astype(jnp.bfloat16)
        return acc + lax.dot_general(stack, stack, NT, preferred_element_type=jnp.float32)

    nine = lax.fori_loop(
        0, fibers // step, gram_step, jnp.zeros((3 * padded, 3 * padded), jnp.float32)
    )
    tall = nine[:padded] + nine[padded:2 * padded] + nine[2 * padded:]
    gram = tall[:, :padded] + tall[:, padded:2 * padded] + tall[:, 2 * padded:]
    gram = jnp.concatenate(
        [gram, jnp.zeros((padded, lanes - padded), jnp.float32)], axis=1
    )
    gram_tile = jnp.concatenate(
        [gram[8 * t:8 * t + 8] for t in range(tiles)], axis=1
    )
    gram_lanes = gram_out.shape[1]
    if gram_lanes > tiles * lanes:
        gram_tile = jnp.concatenate(
            [gram_tile, jnp.zeros((8, gram_lanes - tiles * lanes), jnp.float32)], axis=1
        )
    gram_out[...] = gram_tile
    gram_in[m] = gram_tile
    loads[6].wait()
    for mate in mates[::-1]:
        send(gram_out, gram_in.at[m], 4, (g, mate))

    def turn(f, carry):
        for j in range(4):
            turned[4 * f + j] = precond[4 * f + j].T
        return carry

    lax.fori_loop(0, fibers // 4, turn, 0)

    wait_bytes(leaf_in.at[pl.ds(0, members - 1)], 1)
    wait_bytes(strad_in.at[pl.ds(0, groups - 1)], 3)
    leaf_got = leaf_in[...]
    named = pltpu.roll(leaf_got, cap, 1).reshape(members * 2 * cap, width)[:, :fibers]
    is_row = iota((members * 2 * cap, 1), 0) % (2 * cap) < cap
    leaf_sel = ((named == fiber) & is_row).astype(jnp.float32)
    sel = jnp.concatenate([leaf_sel, strad_sel.astype(jnp.float32)], axis=0)
    got = jnp.concatenate(
        [
            leaf_got.reshape(members * 2 * cap, width),
            strad_in[...].reshape(strad_rows, width),
        ],
        axis=0,
    )
    sel = sel.astype(jnp.bfloat16)
    high, mid, low = split3(got)
    moved = (
        lax.dot_general(sel, high, TN, preferred_element_type=jnp.float32)
        + lax.dot_general(sel, mid, TN, preferred_element_type=jnp.float32)
        + lax.dot_general(sel, low, TN, preferred_element_type=jnp.float32)
    )
    field = basis[(krylov - 1) * fibers:, :] + moved
    field_ref[...] = field.astype(jnp.bfloat16).astype(jnp.float32)

    block = 16
    pieces = []
    sums = [jnp.zeros((8, width), jnp.float32)] * (krylov + 1)
    for t in range(fibers // block):
        tile = field_ref[t * block:(t + 1) * block, :]
        lhs = jnp.concatenate(
            [
                jnp.where(iota((block, width), 0) == j, tile, 0.0).astype(jnp.bfloat16)
                for j in range(block)
            ],
            axis=1,
        )
        rhs = jnp.concatenate([turned[t * block + j] for j in range(block)], axis=0)
        piece = jnp.dot(lhs, rhs, preferred_element_type=jnp.float32)
        pieces.append(piece)
        for k in range(krylov + 1):
            first = k * fibers + t * block
            other = piece if k == krylov else basis[first:first + block, :]
            product = (other * piece).reshape(block // 8, 8, width)
            sums[k] = sums[k] + jnp.sum(product, axis=0)
    applied = jnp.concatenate(pieces, axis=0)
    sums = [jnp.sum(x, axis=0, keepdims=True) for x in sums]
    rows_of = pl.cdiv(krylov + 1, 8) * 8
    sums.append(jnp.zeros((rows_of - krylov - 1, width), jnp.float32))
    column = jnp.sum(jnp.concatenate(sums, axis=0), axis=1, keepdims=True)
    shape = (rows_of, width)
    dots = jnp.sum(
        jnp.where(iota(shape, 0) == iota(shape, 1), column, 0.0), axis=0, keepdims=True
    )
    dots_out[...] = dots
    dots_in[me] = dots
    if devices <= 64:
        for i in range(1, groups * members):
            to = (([g] + peers)[i // members], ([m] + mates)[i % members])
            send(dots_out, dots_in.at[me], 8, to)
    else:

        def send_dots(o, carry):
            to = lax.rem(me + devices - o, devices)
            send(dots_out, dots_in.at[me], 8, (to // members, lax.rem(to, members)))
            return carry

        lax.fori_loop(1, devices, send_dots, 0)

    wait_bytes(gram_in.at[pl.ds(0, members - 1)], 5)
    gram_sum = jnp.sum(gram_in[...], axis=0)
    gram2_out[...] = gram_sum
    gram2_in[g] = gram_sum
    for peer in peers[::-1]:
        send(gram2_out, gram2_in.at[g], 6, (peer, m))

    wait_bytes(gram2_in.at[pl.ds(0, groups - 1)], 7)
    gram_all = jnp.sum(gram2_in[...], axis=0) / total
    wait_bytes(dots_in.at[pl.ds(0, devices - 1)], 9)
    dots = jnp.sum(dots_in[...], axis=0) / total

    lane = iota((1, width), 1)
    coef = jnp.where(lane < krylov, dots, 0.0)
    residual = applied
    for k in range(krylov):
        residual = residual - coef[:, k:k + 1] * basis[k * fibers:(k + 1) * fibers, :]
    square = jnp.sum(
        jnp.where(lane == krylov, dots, 0.0) - 2.0 * coef * coef, axis=1, keepdims=True
    )
    short = coef[:, :lanes]
    wide = jnp.concatenate([short] * (gram_lanes // lanes), axis=1)
    at = iota((8, gram_lanes), 1) // lanes
    down = jnp.zeros((8, gram_lanes), jnp.float32)
    for t in range(tiles):
        shape = (8, width)
        picked = jnp.where(iota(shape, 0) + 8 * t == iota(shape, 1), coef, 0.0)
        down = jnp.where(at == t, jnp.sum(picked, axis=1, keepdims=True), down)
    quad = jnp.sum(gram_all * down * wide, axis=0, keepdims=True)
    square = square + jnp.sum(quad, axis=1, keepdims=True)
    beta = jnp.sqrt(square + EPS)
    coef_ref[...] = jnp.where(lane == krylov, beta, coef)[:, :krylov + 1]
    next_ref[...] = residual / beta

    wait_bytes(leaf_out.at[pl.ds(0, members - 1)], 0)
    wait_bytes(strad_out.at[pl.ds(0, groups - 1)], 2)
    wait_bytes(gram_in.at[pl.ds(0, members - 1)], 4)
    wait_bytes(gram2_in.at[pl.ds(0, groups - 1)], 6)
    wait_bytes(dots_in.at[pl.ds(0, devices - 1)], 8)


def put_out(coef_ref, next_ref, coef_h, next_h, sem):
    second = pltpu.make_async_copy(next_ref, next_h, sem.at[1])
    first = pltpu.make_async_copy(coef_ref, coef_h, sem.at[0])
    second.start()
    first.start()
    first.wait()
    second.wait()


def local(basis, precond, leaf_rows, leaf_fiber, strad_rows, strad_fiber, strad_count):
    groups = lax.axis_size("grp")
    members = lax.axis_size("mem")
    devices = groups * members
    krylov, fibers, width = basis.shape
    cap = leaf_rows.shape[0] // members
    slots = strad_rows.shape[0] // groups
    tiles = pl.cdiv(krylov, 8)
    lanes = 1 << (tiles * 8 - 1).bit_length()
    gram_lanes = pl.cdiv(tiles * lanes, 128) * 128
    f32, i32 = jnp.float32, jnp.int32
    any_space = pl.BlockSpec(memory_space=pl.ANY)
    vmem = pl.BlockSpec(memory_space=pltpu.VMEM)
    coeffs, vector = pl.pallas_call(
        functools.partial(
            kernel, groups, members, krylov, fibers, float(fibers * width * devices)
        ),
        out_shape=(
            pltpu.VMEM((1, krylov + 1), f32),
            pltpu.VMEM((fibers, width), f32),
        ),
        in_specs=[any_space] * 7,
        out_specs=(vmem, vmem),
        scratch_shapes=[
            pltpu.VMEM((krylov * fibers, width), f32),
            pltpu.VMEM(precond.shape, precond.dtype),
            pltpu.VMEM(leaf_rows.shape, f32),
            pltpu.VMEM((1, leaf_fiber.shape[0]), i32),
            pltpu.VMEM(strad_rows.shape, f32),
            pltpu.VMEM((1, strad_fiber.shape[0]), i32),
            pltpu.VMEM(strad_count.shape, i32),
            pltpu.VMEM((members, 2 * cap, width), f32),
            pltpu.VMEM((members, 2 * cap, width), f32),
            pltpu.VMEM((groups, slots, width), f32),
            pltpu.VMEM((groups, slots, width), f32),
            pltpu.VMEM((8, gram_lanes), f32),
            pltpu.VMEM((members, 8, gram_lanes), f32),
            pltpu.VMEM((8, gram_lanes), f32),
            pltpu.VMEM((groups, 8, gram_lanes), f32),
            pltpu.VMEM((1, width), f32),
            pltpu.VMEM((devices, 1, width), f32),
            pltpu.VMEM((fibers, width), f32),
            pltpu.VMEM(precond.shape, precond.dtype),
            pltpu.SemaphoreType.DMA((7,)),
            pltpu.SemaphoreType.DMA((10,)),
        ],
        compiler_params=pltpu.CompilerParams(collective_id=0, has_side_effects=True),
        name="gmres_step",
    )(
        basis.reshape(krylov * fibers, width), precond, leaf_rows,
        leaf_fiber.reshape(1, -1), strad_rows, strad_fiber.reshape(1, -1), strad_count,
    )
    coeffs, vector = pl.pallas_call(
        put_out,
        out_shape=(
            jax.ShapeDtypeStruct((1, krylov + 1), f32),
            jax.ShapeDtypeStruct((fibers, width), f32),
        ),
        in_specs=[vmem, vmem],
        out_specs=(any_space, any_space),
        scratch_shapes=[pltpu.SemaphoreType.DMA((2,))],
        compiler_params=pltpu.CompilerParams(vmem_limit_bytes=1 << 20),
        name="put_out",
    )(coeffs, vector)
    return coeffs.reshape(krylov + 1), vector


def solution(mesh):
    return jax.shard_map(
        local,
        mesh=mesh,
        in_specs=(
            P(None, ("grp", "mem"), None),
            P(("grp", "mem"), None, None),
            P(("grp", "mem"), None),
            P(("grp", "mem")),
            P(("grp", "mem"), None),
            P(("grp", "mem")),
            P(("grp", "mem"), None),
        ),
        out_specs=(P(), P(("grp", "mem"), None)),
        check_vma=False,
    )
```

```python
import functools

import jax
import jax.numpy as jnp
from jax import lax
from jax.experimental import pallas as pl
from jax.experimental.pallas import tpu as pltpu
from jax.sharding import PartitionSpec as P

EPS = 1e-06
MESH = pl.DeviceIdType.MESH
NT = (((1,), (1,)), ((), ()))
TN = (((0,), (0,)), ((), ()))


def iota(shape, axis):
    return lax.broadcasted_iota(jnp.int32, shape, axis)


def row_to_column(row, rows):
    shape = (rows, row.shape[1])
    diagonal = iota(shape, 0) == iota(shape, 1)
    return jnp.sum(jnp.where(diagonal, row, 0.0), axis=1, keepdims=True)


def split3(x):
    high = x.astype(jnp.bfloat16)
    rest = x - high.astype(jnp.float32)
    mid = rest.astype(jnp.bfloat16)
    low = (rest - mid.astype(jnp.float32)).astype(jnp.bfloat16)
    return high, mid, low


def kernel(
    groups, members, krylov, fibers, total,
    basis_h, precond_h, leaf_h, leaf_id_h, strad_h, strad_id_h, count_h,
    coef_ref, next_ref,
    basis, precond, leaf, leaf_id, strad, strad_id, count,
    leaf_out, leaf_in, strad_out, strad_in,
    gram_out, gram_in, gram2_out, gram2_in, dots_out, dots_in,
    field_ref, turned, local_sem, sem,
):
    g, m = lax.axis_index("grp"), lax.axis_index("mem")
    devices = groups * members
    me = g * members + m
    width = basis.shape[1]
    cap = leaf.shape[0] // members
    slots = strad.shape[0] // groups

    barrier = pltpu.get_barrier_semaphore()
    mates = [lax.rem(m + o, members) for o in range(1, members)]
    peers = [lax.rem(g + o, groups) for o in range(1, groups)]
    for peer in peers:
        pl.semaphore_signal(barrier, inc=1, device_id=(peer, m), device_id_type=MESH)
    for mate in mates:
        pl.semaphore_signal(barrier, inc=1, device_id=(g, mate), device_id_type=MESH)

    loads = [
        pltpu.make_async_copy(src, dst, local_sem.at[i])
        for i, (src, dst) in enumerate(
            [
                (leaf_h, leaf), (leaf_id_h, leaf_id), (strad_h, strad),
                (count_h, count), (strad_id_h, strad_id),
                (basis_h, basis.at[pl.ds(0, krylov * fibers)]), (precond_h, precond),
            ]
        )
    ]
    for load in loads:
        load.start()
    for load in loads[:5]:
        load.wait()

    leaf_rows = leaf.shape[0]
    ids = jnp.broadcast_to(
        row_to_column(leaf_id[...].astype(jnp.float32), leaf_rows), (leaf_rows, width)
    )
    rows = leaf[...]
    for d in range(members):
        leaf_out[d, :cap, :] = rows[d * cap:(d + 1) * cap]
        leaf_out[d, cap:, :] = ids[d * cap:(d + 1) * cap]
    strad_rows = strad.shape[0]
    shape = (strad_rows, groups)
    of_group = iota(shape, 0) // slots == iota(shape, 1)
    live = jnp.sum(
        jnp.where(of_group, count[...].astype(jnp.float32), 0.0), axis=1, keepdims=True
    )
    within = (iota((strad_rows, 1), 0) % slots).astype(jnp.float32)
    kept = jnp.where(within < live, strad[...], 0.0)
    strad_out[...] = kept.reshape(groups, slots, width)
    leaf_in[m] = leaf_out[m]
    strad_in[g] = strad_out[g]
    strad_column = row_to_column(strad_id[...].astype(jnp.float32), strad_rows)
    fiber = iota((1, fibers), 1).astype(jnp.float32)
    strad_sel = (strad_column == fiber).astype(jnp.bfloat16)

    pl.semaphore_wait(barrier, members - 1 + groups - 1)

    def send(src, dst, pair, device):
        pltpu.make_async_remote_copy(
            src_ref=src, dst_ref=dst, send_sem=sem.at[pair], recv_sem=sem.at[pair + 1],
            device_id=device, device_id_type=MESH,
        ).start()

    def wait_bytes(ref, i):
        pltpu.make_async_copy(ref, ref, sem.at[i]).wait()

    for peer in peers[::-1]:
        send(strad_out.at[peer], strad_in.at[g], 2, (peer, m))
    for mate in mates[::-1]:
        send(leaf_out.at[mate], leaf_in.at[m], 0, (g, mate))

    loads[5].wait()
    step = 8
    tiles = pl.cdiv(krylov, 8)
    padded = tiles * 8
    lanes = 1 << (padded - 1).bit_length()

    def gram_step(c, acc):
        parts = []
        for j in range(step):
            x = basis[pl.ds(c * step + j, krylov, stride=fibers), :]
            x = jnp.concatenate(
                [x, jnp.zeros((padded - krylov, width), jnp.float32)], axis=0
            )
            parts.append(x)
        x = jnp.concatenate(parts, axis=1)
        high, mid, low = split3(x)
        stack = jnp.concatenate(
            [high.astype(jnp.float32), mid.astype(jnp.float32), low.astype(jnp.float32)], axis=0
        ).astype(jnp.bfloat16)
        return acc + lax.dot_general(stack, stack, NT, preferred_element_type=jnp.float32)

    nine = lax.fori_loop(
        0, fibers // step, gram_step, jnp.zeros((3 * padded, 3 * padded), jnp.float32)
    )
    tall = nine[:padded] + nine[padded:2 * padded] + nine[2 * padded:]
    gram = tall[:, :padded] + tall[:, padded:2 * padded] + tall[:, 2 * padded:]
    gram = jnp.concatenate(
        [gram, jnp.zeros((padded, lanes - padded), jnp.float32)], axis=1
    )
    gram_tile = jnp.concatenate(
        [gram[8 * t:8 * t + 8] for t in range(tiles)], axis=1
    )
    gram_lanes = gram_out.shape[1]
    if gram_lanes > tiles * lanes:
        gram_tile = jnp.concatenate(
            [gram_tile, jnp.zeros((8, gram_lanes - tiles * lanes), jnp.float32)], axis=1
        )
    gram_out[...] = gram_tile
    gram_in[m] = gram_tile
    loads[6].wait()
    for mate in mates[::-1]:
        send(gram_out, gram_in.at[m], 4, (g, mate))

    def turn(f, carry):
        for j in range(4):
            turned[4 * f + j] = precond[4 * f + j].T
        return carry

    lax.fori_loop(0, fibers // 4, turn, 0)

    wait_bytes(leaf_in.at[pl.ds(0, members - 1)], 1)
    wait_bytes(strad_in.at[pl.ds(0, groups - 1)], 3)
    leaf_got = leaf_in[...]
    named = pltpu.roll(leaf_got, cap, 1).reshape(members * 2 * cap, width)[:, :fibers]
    is_row = iota((members * 2 * cap, 1), 0) % (2 * cap) < cap
    leaf_sel = ((named == fiber) & is_row).astype(jnp.float32)
    sel = jnp.concatenate([leaf_sel, strad_sel.astype(jnp.float32)], axis=0)
    got = jnp.concatenate(
        [
            leaf_got.reshape(members * 2 * cap, width),
            strad_in[...].reshape(strad_rows, width),
        ],
        axis=0,
    )
    sel = sel.astype(jnp.bfloat16)
    high, mid, low = split3(got)
    moved = (
        lax.dot_general(sel, high, TN, preferred_element_type=jnp.float32)
        + lax.dot_general(sel, mid, TN, preferred_element_type=jnp.float32)
        + lax.dot_general(sel, low, TN, preferred_element_type=jnp.float32)
    )
    field = basis[(krylov - 1) * fibers:krylov * fibers, :] + moved
    field_ref[...] = field.astype(jnp.bfloat16).astype(jnp.float32)

    block = 16
    pieces = []
    sums = [jnp.zeros((8, width), jnp.float32)] * (krylov + 1)
    for t in range(fibers // block):
        tile = field_ref[t * block:(t + 1) * block, :]
        lhs = jnp.concatenate(
            [
                jnp.where(iota((block, width), 0) == j, tile, 0.0).astype(jnp.bfloat16)
                for j in range(block)
            ],
            axis=1,
        )
        rhs = jnp.concatenate([turned[t * block + j] for j in range(block)], axis=0)
        piece = jnp.dot(lhs, rhs, preferred_element_type=jnp.float32)
        pieces.append(piece)
        for k in range(krylov + 1):
            first = k * fibers + t * block
            other = piece if k == krylov else basis[first:first + block, :]
            product = (other * piece).reshape(block // 8, 8, width)
            sums[k] = sums[k] + jnp.sum(product, axis=0)
    applied = jnp.concatenate(pieces, axis=0)
    sums = [jnp.sum(x, axis=0, keepdims=True) for x in sums]
    rows_of = pl.cdiv(krylov + 1, 8) * 8
    sums.append(jnp.zeros((rows_of - krylov - 1, width), jnp.float32))
    column = jnp.sum(jnp.concatenate(sums, axis=0), axis=1, keepdims=True)
    shape = (rows_of, width)
    dots = jnp.sum(
        jnp.where(iota(shape, 0) == iota(shape, 1), column, 0.0), axis=0, keepdims=True
    )
    dots_out[...] = dots
    dots_in[me] = dots
    if devices <= 64:
        for i in range(1, groups * members):
            to = (([g] + peers)[i // members], ([m] + mates)[i % members])
            send(dots_out, dots_in.at[me], 8, to)
    else:

        def send_dots(o, carry):
            to = lax.rem(me + devices - o, devices)
            send(dots_out, dots_in.at[me], 8, (to // members, lax.rem(to, members)))
            return carry

        lax.fori_loop(1, devices, send_dots, 0)

    wait_bytes(gram_in.at[pl.ds(0, members - 1)], 5)
    gram_sum = jnp.sum(gram_in[...], axis=0)
    gram2_out[...] = gram_sum
    gram2_in[g] = gram_sum
    for peer in peers[::-1]:
        send(gram2_out, gram2_in.at[g], 6, (peer, m))

    wait_bytes(gram2_in.at[pl.ds(0, groups - 1)], 7)
    gram_all = jnp.sum(gram2_in[...], axis=0) / total
    wait_bytes(dots_in.at[pl.ds(0, devices - 1)], 9)
    dots = jnp.sum(dots_in[...], axis=0) / total

    lane = iota((1, width), 1)
    coef = jnp.where(lane < krylov, dots, 0.0)
    residual = applied
    for k in range(krylov):
        residual = residual - coef[:, k:k + 1] * basis[k * fibers:(k + 1) * fibers, :]
    square = jnp.sum(
        jnp.where(lane == krylov, dots, 0.0) - 2.0 * coef * coef, axis=1, keepdims=True
    )
    short = coef[:, :lanes]
    wide = jnp.concatenate([short] * (gram_lanes // lanes), axis=1)
    at = iota((8, gram_lanes), 1) // lanes
    down = jnp.zeros((8, gram_lanes), jnp.float32)
    for t in range(tiles):
        shape = (8, width)
        picked = jnp.where(iota(shape, 0) + 8 * t == iota(shape, 1), coef, 0.0)
        down = jnp.where(at == t, jnp.sum(picked, axis=1, keepdims=True), down)
    quad = jnp.sum(gram_all * down * wide, axis=0, keepdims=True)
    square = square + jnp.sum(quad, axis=1, keepdims=True)
    beta = jnp.sqrt(square + EPS)
    coef_ref[...] = jnp.where(lane == krylov, beta, coef)[:, :krylov + 1]
    next_ref[...] = residual / beta

    wait_bytes(leaf_out.at[pl.ds(0, members - 1)], 0)
    wait_bytes(strad_out.at[pl.ds(0, groups - 1)], 2)
    wait_bytes(gram_in.at[pl.ds(0, members - 1)], 4)
    wait_bytes(gram2_in.at[pl.ds(0, groups - 1)], 6)
    wait_bytes(dots_in.at[pl.ds(0, devices - 1)], 8)


def put_out(coef_ref, next_ref, coef_h, next_h, sem):
    second = pltpu.make_async_copy(next_ref, next_h, sem.at[1])
    first = pltpu.make_async_copy(coef_ref, coef_h, sem.at[0])
    second.start()
    first.start()
    first.wait()
    second.wait()


def local(basis, precond, leaf_rows, leaf_fiber, strad_rows, strad_fiber, strad_count):
    groups = lax.axis_size("grp")
    members = lax.axis_size("mem")
    devices = groups * members
    krylov, fibers, width = basis.shape
    cap = leaf_rows.shape[0] // members
    slots = strad_rows.shape[0] // groups
    tiles = pl.cdiv(krylov, 8)
    lanes = 1 << (tiles * 8 - 1).bit_length()
    gram_lanes = pl.cdiv(tiles * lanes, 128) * 128
    f32, i32 = jnp.float32, jnp.int32
    any_space = pl.BlockSpec(memory_space=pl.ANY)
    vmem = pl.BlockSpec(memory_space=pltpu.VMEM)
    coeffs, vector = pl.pallas_call(
        functools.partial(
            kernel, groups, members, krylov, fibers, float(fibers * width * devices)
        ),
        out_shape=(
            pltpu.VMEM((1, krylov + 1), f32),
            pltpu.VMEM((fibers, width), f32),
        ),
        in_specs=[any_space] * 7,
        out_specs=(vmem, vmem),
        scratch_shapes=[
            pltpu.VMEM((tiles * 8 * fibers, width), f32),
            pltpu.VMEM(precond.shape, precond.dtype),
            pltpu.VMEM(leaf_rows.shape, f32),
            pltpu.VMEM((1, leaf_fiber.shape[0]), i32),
            pltpu.VMEM(strad_rows.shape, f32),
            pltpu.VMEM((1, strad_fiber.shape[0]), i32),
            pltpu.VMEM(strad_count.shape, i32),
            pltpu.VMEM((members, 2 * cap, width), f32),
            pltpu.VMEM((members, 2 * cap, width), f32),
            pltpu.VMEM((groups, slots, width), f32),
            pltpu.VMEM((groups, slots, width), f32),
            pltpu.VMEM((8, gram_lanes), f32),
            pltpu.VMEM((members, 8, gram_lanes), f32),
            pltpu.VMEM((8, gram_lanes), f32),
            pltpu.VMEM((groups, 8, gram_lanes), f32),
            pltpu.VMEM((1, width), f32),
            pltpu.VMEM((devices, 1, width), f32),
            pltpu.VMEM((fibers, width), f32),
            pltpu.VMEM(precond.shape, precond.dtype),
            pltpu.SemaphoreType.DMA((7,)),
            pltpu.SemaphoreType.DMA((10,)),
        ],
        compiler_params=pltpu.CompilerParams(collective_id=0, has_side_effects=True),
        name="gmres_step",
    )(
        basis.reshape(krylov * fibers, width), precond, leaf_rows,
        leaf_fiber.reshape(1, -1), strad_rows, strad_fiber.reshape(1, -1), strad_count,
    )
    coeffs, vector = pl.pallas_call(
        put_out,
        out_shape=(
            jax.ShapeDtypeStruct((1, krylov + 1), f32),
            jax.ShapeDtypeStruct((fibers, width), f32),
        ),
        in_specs=[vmem, vmem],
        out_specs=(any_space, any_space),
        scratch_shapes=[pltpu.SemaphoreType.DMA((2,))],
        compiler_params=pltpu.CompilerParams(vmem_limit_bytes=1 << 20),
        name="put_out",
    )(coeffs, vector)
    return coeffs.reshape(krylov + 1), vector


def solution(mesh):
    return jax.shard_map(
        local,
        mesh=mesh,
        in_specs=(
            P(None, ("grp", "mem"), None),
            P(("grp", "mem"), None, None),
            P(("grp", "mem"), None),
            P(("grp", "mem")),
            P(("grp", "mem"), None),
            P(("grp", "mem")),
            P(("grp", "mem"), None),
        ),
        out_specs=(P(), P(("grp", "mem"), None)),
        check_vma=False,
    )
```
